32 devices in a mesh: fsdp: 2 (over y), tensor: 4 (over x, core), replica: 4 (over z).
Axes of the slice: x: 2, y: 2, z: 4, core: 2. Of those that a mesh axis runs over, the one named last changes fastest.
Arguments:
- gradient: bfloat16 [4, 4096, 8192], P('replica', 'fsdp', 'tensor'), may hold values from -400 to 400, as said below
- momentum: float32 [4, 4096, 8192], P('replica', 'fsdp', 'tensor'), may hold values from -6 to 6
- basis: float32 [8192, 256], P('tensor', 'fsdp'), may hold values from -0.0625 to 0.0625
Outputs:
- update: bfloat16 [4096, 8192], P('fsdp', 'tensor')
- momentum_new: float32 [4, 4096, 8192], P('replica', 'fsdp', 'tensor')
- basis_new: float32 [8192, 256], P('tensor', 'fsdp')
The draws below stay inside these ranges and needn't reach their ends.
Inputs may be any that keep to these rules, and one draw needn't show every extreme that they name: gradient entries are finite real numbers.
All inputs are finite; a program needn't handle non-finite values.
Results may differ from the reference program's by a relative error of at most 0.001.
Values sent between devices are 32-bit elements; how exact they have to be, the bound alone decides.
A program may use at most 128 MiB of HBM per device.

```python
import math
import jax
import jax.numpy as jnp
from jax import lax

M_ROWS = 4096
NCOLS = 8192
RANK = 256
REPL = 4


def draw_gradient(key, part):
    key_rows, key_cols, key_own = jax.random.split(key, 3)
    rows = jnp.exp(jax.random.uniform(key_rows, (1, M_ROWS, 1), jnp.float32) * math.log(10.0))
    rising = jnp.exp(jnp.arange(NCOLS, dtype=jnp.float32) / NCOLS * math.log(3.0))
    rough = jnp.exp(jax.random.uniform(key_cols, (NCOLS,), jnp.float32, -math.log(2.0), math.log(2.0)))
    cols = (rising * rough).reshape(1, 1, NCOLS)
    base = jax.random.truncated_normal(key_own, -6.0, 6.0, (REPL, M_ROWS, NCOLS), jnp.float32)
    return (base * rows * cols).astype(jnp.bfloat16)


def steps_of(rng, dims, pieces, smallest, largest):
    gain = 1.0
    for position, shards_of in pieces:
        draws = jax.random.uniform(jax.random.fold_in(jax.random.fold_in(rng, 6), position), (shards_of,), jnp.float32, smallest / len(pieces), largest / len(pieces))
        gain = gain * jnp.repeat(jnp.exp(draws), dims[position] // shards_of).reshape((-1,) + (1,) * (len(dims) - 1 - position))
    return gain


def noise(stream_key, shape, scale, most, shards=(), kind=jnp.bfloat16):
    level = steps_of(stream_key, shape, shards, -0.22, 0.18) if shards else 1.0
    array = jax.random.normal(stream_key, shape, jnp.float32) * scale * level
    return jnp.minimum(jnp.maximum(array, -most), most).astype(kind)


def setup_inputs(seed: int = 0) -> dict:
    arg_keys = jax.random.split(jax.random.key(seed), 4)
    return {
        "gradient": draw_gradient(jax.random.fold_in(arg_keys[3], 71), 0),
        "momentum": noise(arg_keys[1], (REPL, M_ROWS, NCOLS), 1.0, 6.0, ((0, 4), (1, 2), (2, 4)), jnp.float32),
        "basis": noise(arg_keys[2], (NCOLS, RANK), NCOLS ** -0.5, 0.0625, ((0, 4), (1, 2)), jnp.float32),
    }


HIGH = lax.Precision.HIGHEST

def reference(gradient, momentum, basis):
    count = gradient.shape[0]

    def left_term(index):
        buffer = momentum[index] + gradient[index].astype(jnp.float32)
        return jnp.dot(buffer.astype(jnp.float32), basis.astype(jnp.float32), precision=HIGH, preferred_element_type=jnp.float32)
    left = lax.optimization_barrier(jnp.sum(lax.map(left_term, jnp.arange(count)), axis=0)) / count
    gram = jnp.dot(left.T.astype(jnp.float32), left.astype(jnp.float32), precision=HIGH, preferred_element_type=jnp.float32)
    chol = jnp.linalg.cholesky(gram)
    ortho = lax.linalg.triangular_solve(chol, left, left_side=False, lower=True, transpose_a=True)

    def right_term(index):
        buffer = momentum[index] + gradient[index].astype(jnp.float32)
        return jnp.dot(buffer.T.astype(jnp.float32), ortho.astype(jnp.float32), precision=HIGH, preferred_element_type=jnp.float32)
    right = lax.optimization_barrier(jnp.sum(lax.map(right_term, jnp.arange(count)), axis=0)) / count
    norms = jnp.sqrt(lax.optimization_barrier(jnp.sum(right * right, axis=0)) + 1e-12)
    basis_new = right / norms
    lowrank = jnp.dot(ortho.astype(jnp.float32), right.T.astype(jnp.float32), precision=HIGH, preferred_element_type=jnp.float32)

    def feedback(index):
        buffer = momentum[index] + gradient[index].astype(jnp.float32)
        return buffer - 0.05 * lowrank
    momentum_new = lax.map(feedback, jnp.arange(count))
    scale = (M_ROWS * NCOLS / RANK) ** 0.5
    update = (scale * jnp.dot(ortho.astype(jnp.float32), basis_new.T.astype(jnp.float32), precision=HIGH, preferred_element_type=jnp.float32)).astype(jnp.bfloat16)
    return (update, momentum_new, basis_new)
```

```python
import jax
import jax.numpy as jnp
from jax import lax
from jax.experimental import pallas as pl
from jax.experimental.pallas import tpu as pltpu
from jax.sharding import PartitionSpec as P

HIGHEST = lax.Precision.HIGHEST
HIGH = lax.Precision.HIGH
BLOCK = 16


def mm(a, b, precision):
    return jnp.dot(a, b, precision=precision, preferred_element_type=jnp.float32)


def pick(parts, index):
    return lax.dynamic_index_in_dim(parts, index, 0, keepdims=False)


def shift(x, axis, step):
    n = lax.axis_size(axis)
    return lax.ppermute(x, axis, [(i, (i + step) % n) for i in range(n)])


def swap(x, axis, bit):
    n = lax.axis_size(axis)
    return lax.ppermute(x, axis, [(i, i ^ bit) for i in range(n)])


def bits_of(axis):
    n = lax.axis_size(axis)
    bits, bit = [], 1
    while bit < n:
        bits.append(bit)
        bit *= 2
    return bits


def halve(x, axis, bits):
    for bit in bits:
        upper = (lax.axis_index(axis) // bit) % 2
        parts = x.reshape(2, x.shape[0] // 2, x.shape[1])
        x = pick(parts, upper) + swap(pick(parts, 1 - upper), axis, bit)
    return x


def double(x, axis, bits):
    for bit in reversed(bits):
        upper = (lax.axis_index(axis) // bit) % 2 == 1
        other = swap(x, axis, bit)
        x = jnp.concatenate([jnp.where(upper, other, x), jnp.where(upper, x, other)], axis=0)
    return x


def ring_scatter(x, axis):
    n = lax.axis_size(axis)
    me = lax.axis_index(axis)
    parts = x.reshape(n, 2, x.shape[0] // (2 * n), x.shape[1])
    up, down = parts[:, 0], parts[:, 1]
    a, b = pick(up, (me + n - 1) % n), pick(down, (me + 1) % n)
    for step in range(n - 1):
        a = shift(a, axis, 1) + pick(up, (me + 2 * n - step - 2) % n)
        b = shift(b, axis, n - 1) + pick(down, (me + step + 2) % n)
    return jnp.concatenate([a, b], axis=0)


def ring_gather(x, axis):
    n = lax.axis_size(axis)
    me = lax.axis_index(axis)
    half = x.shape[0] // 2
    a, b = x[:half], x[half:]
    out = jnp.zeros((n, 2, half, x.shape[1]), x.dtype)

    def put(out, value, chunk, side):
        return lax.dynamic_update_slice(out, value[None, None], (chunk, side, 0, 0))

    out = put(put(out, a, me, 0), b, me, 1)
    for step in range(n - 1):
        a = shift(a, axis, 1)
        b = shift(b, axis, n - 1)
        out = put(out, a, (me + n - step - 1) % n, 0)
        out = put(out, b, (me + step + 1) % n, 1)
    return out.reshape(n * x.shape[0], x.shape[1])


def sum_over(x, axis, bits, ring):
    half = x.shape[0] // 2
    first = ring_scatter(halve(x[:half], axis, bits), ring)
    second = halve(ring_scatter(x[half:], ring), axis, bits)
    first = double(ring_gather(first, ring), axis, bits)
    second = ring_gather(double(second, axis, bits), ring)
    return jnp.concatenate([first, second], axis=0)


def invert_kernel(gram_ref, out_ref, work):
    size = gram_ref.shape[0]
    rows = lax.broadcasted_iota(jnp.int32, (size, size), 0)
    cols = lax.broadcasted_iota(jnp.int32, (size, size), 1)
    work[:, :size] = gram_ref[...]
    work[:, size:] = jnp.where(rows == cols, 1.0, 0.0).astype(jnp.float32)
    lane = lax.broadcasted_iota(jnp.int32, (BLOCK, 2 * size), 1)
    row = lax.broadcasted_iota(jnp.int32, (BLOCK, 2 * size), 0)
    below = lax.broadcasted_iota(jnp.int32, (BLOCK, 1), 0)
    for start in range(0, size, BLOCK):
        panel = work[start : start + BLOCK, :]
        for j in range(BLOCK):
            column = start + j
            factor = panel[:, column : column + 1] / panel[j : j + 1, column : column + 1]
            factor = jnp.where(below > j, factor, 0.0)
            panel = panel - factor * panel[j : j + 1, :]
        pivots = jnp.sum(jnp.where(lane == row + start, panel, 0.0), axis=1, keepdims=True)
        panel = panel / jnp.sqrt(pivots)
        out_ref[start : start + BLOCK, :] = panel[:, size:]
        if start + BLOCK < size:
            outer = lax.dot_general(
                panel[:, :size],
                panel,
                (((0,), (0,)), ((), ())),
                precision=HIGHEST,
                preferred_element_type=jnp.float32,
            )
            work[start + BLOCK :, :] = work[start + BLOCK :, :] - outer[start + BLOCK :, :]


def inverse_factor(gram, interpret=False):
    size = gram.shape[0]
    return pl.pallas_call(
        invert_kernel,
        out_shape=jax.ShapeDtypeStruct((size, size), jnp.float32),
        in_specs=[pl.BlockSpec(memory_space=pltpu.VMEM)],
        out_specs=pl.BlockSpec(memory_space=pltpu.VMEM),
        scratch_shapes=[pltpu.VMEM((size, 2 * size), jnp.float32)],
        interpret=interpret,
    )(gram)


def gather_columns(x, axis):
    for bit in bits_of(axis):
        upper = (lax.axis_index(axis) // bit) % 2 == 1
        other = swap(x, axis, bit)
        x = jnp.concatenate([jnp.where(upper, other, x), jnp.where(upper, x, other)], axis=1)
    return x


def local(gradient, momentum, basis):
    replicas = lax.axis_size("replica")
    rank_local = basis.shape[1]
    rank = rank_local * lax.axis_size("fsdp")
    rows = gradient.shape[1] * lax.axis_size("fsdp")
    columns = gradient.shape[2] * lax.axis_size("tensor")
    buffer = momentum[0] + gradient[0].astype(jnp.float32)

    left = mm(buffer, gather_columns(basis, "fsdp"), HIGH)
    bits = bits_of("tensor")
    left = halve(left, "tensor", bits[:1])
    left = sum_over(left, "tensor", bits[1:], "replica")
    left = double(left, "tensor", bits[:1]) / replicas

    gram = mm(left.T, left, HIGHEST)
    for bit in bits_of("fsdp"):
        gram = gram + swap(gram, "fsdp", bit)
    ortho = mm(left, inverse_factor(gram).T, HIGHEST)

    right = mm(buffer.T, ortho, HIGH)
    right = sum_over(right, "fsdp", bits_of("fsdp"), "replica") / replicas
    squares = jnp.sum(right * right, axis=0, keepdims=True)
    for bit in bits_of("tensor"):
        squares = squares + swap(squares, "tensor", bit)
    norms = jnp.sqrt(squares + 1e-12)
    basis_full = right / norms
    lowrank = mm(ortho, right.T, lax.Precision.DEFAULT)
    momentum_new = (buffer - 0.05 * lowrank)[None]
    scale = (rows * columns / rank) ** 0.5
    update = (scale * mm(ortho, basis_full.T, HIGH)).astype(jnp.bfloat16)
    offset = lax.axis_index("fsdp") * rank_local
    basis_new = lax.dynamic_slice_in_dim(basis_full, offset, rank_local, 1)
    return (update, momentum_new, basis_new)


def solution(mesh):
    return jax.shard_map(
        local,
        mesh=mesh,
        in_specs=(
            P("replica", "fsdp", "tensor"),
            P("replica", "fsdp", "tensor"),
            P("tensor", "fsdp"),
        ),
        out_specs=(P("fsdp", "tensor"), P("replica", "fsdp", "tensor"), P("tensor", "fsdp")),
        check_vma=False,
    )
```
